512 devices in a mesh: dp: 8 (over z_hi, core), seq: 64 (over z_lo, y, x).
Axes of the slice: x: 4, y: 8, z: 8 (z_hi: 4, z_lo: 2; z = z_hi * 2 + z_lo), core: 2. Of those that a mesh axis runs over, the one named last changes fastest.
Arguments:
- qkv: bfloat16 [8, 64, 128, 1728], P('dp', 'seq'), may hold values from -7 to 7
- segment_ids: int32 [8, 64], P('dp'), may hold values from 0 to 3, never falling along the last dimension, each value on 1 to 32 neighbouring positions
- upstream: bfloat16 [8, 64, 128, 1152], P('dp', 'seq'), may hold values from -6 to 6
- out_weight: bfloat16 [576, 1152], P('dp'), may hold values from -0.25 to 0.25
Outputs:
- output: bfloat16 [8, 64, 128, 1152], P('dp', 'seq')
- qkv_grad: bfloat16 [8, 64, 128, 1728], P('dp', 'seq')
- weight_grad: float32 [576, 1152], P('dp')
The draws below stay inside these ranges and needn't reach their ends.
Inputs may be any that keep to these rules, and one draw needn't show every extreme that they name: `segment_ids`: within a clip the id never falls from one frame to the next; a segment covers at most 32 frames and one segment of every clip covers exactly that many.
All inputs are finite; a program needn't handle non-finite values.
Results may differ from the reference program's by a relative error of at most 0.006.
Values may be sent and summed in bfloat16 or wider, within the bound.
A program may use at most 64 MiB of HBM per device.

```python
import math
import jax
import jax.numpy as jnp
import numpy as np
from jax import lax

D = 1152
HEAD_DIM = 72
HEADS = 8
FRAMES = 64
POS = 128
INNER = 576
CLIPS_ALL = 8
TOKENS_ALL = 65536


def draw_qkv(key, part):
    first = jax.random.fold_in(key, 0)
    full_shape = (CLIPS_ALL, FRAMES, POS, 3, HEADS, HEAD_DIM)
    values_all = jnp.clip(jax.random.normal(first, full_shape, jnp.float32), -6.0, 6.0)
    return values_all.reshape(CLIPS_ALL, FRAMES, POS, 3 * HEADS * HEAD_DIM).astype(jnp.bfloat16)


def levels(own_key, shape, cuts, low, top_value):
    factor_of, own = 1.0, jax.random.fold_in(own_key, 6)
    for dim, blocks in cuts:
        steps = jnp.exp(jax.random.uniform(jax.random.fold_in(own, dim), (blocks,), jnp.float32, low / len(cuts), top_value / len(cuts)))
        factor_of = factor_of * jnp.repeat(steps, shape[dim] // blocks).reshape([-1 if axis == dim else 1 for axis in range(len(shape))])
    return factor_of


def profile(amount, total, limit, skew):
    weights = [(1 << 20) // math.isqrt(rank ** skew) + 1 for rank in range(2, amount + 1)]
    rest, counts = total - limit - (amount - 1), [1] * (amount - 1)
    while rest > 0:
        movable = [i for i in range(amount - 1) if counts[i] < limit]
        mass, left = sum([weights[i] for i in movable]), rest
        for i in movable:
            more = min(limit - counts[i], max(1, left * weights[i] // mass), rest)
            counts[i] = counts[i] + more
            rest = rest - more
    return np.array([limit] + counts)


def ragged(key, amount, total, most, slope):
    if amount == 2:
        one = jax.random.randint(key, (), max(1, total - most), min(most, total - 1) + 1)
        return jnp.stack([one, total - one])
    sizes = jnp.asarray(profile(amount, total, most, slope), jnp.int32)
    pairs = (amount - 1) // 2
    source_of, sink = sizes[1:1 + 2 * pairs:2], sizes[2:2 + 2 * pairs:2]
    room = jnp.minimum(source_of - 1, most - sink)
    passed = jax.random.randint(jax.random.fold_in(key, 1), (pairs,), 0, 1 << 20) % (room + 1)
    sizes = sizes.at[1:1 + 2 * pairs:2].set(source_of - passed).at[2:2 + 2 * pairs:2].set(sink + passed)
    return sizes[jax.random.permutation(jax.random.fold_in(key, 2), amount)]


def scatter_about(key, shape, spread, most, pieces=(), dtype=jnp.bfloat16):
    drawn = jax.random.normal(key, shape, jnp.float32) * spread
    if len(pieces) > 0:
        drawn = levels(key, shape, pieces, -0.22, 0.18) * drawn
    return jnp.clip(drawn, min=-most, max=most).astype(dtype)


def setup_inputs(seed: int = 0) -> dict:
    key_of = jax.random.split(jax.random.key(seed), 5)
    return {
        "qkv": draw_qkv(jax.random.fold_in(key_of[4], 71), 0),
        "segment_ids": jax.vmap(lambda own: jnp.searchsorted(jnp.cumsum(ragged(own, 4, FRAMES, FRAMES // 2, 0)), jnp.arange(FRAMES), side="right"))(jax.random.split(key_of[1], CLIPS_ALL)).reshape((CLIPS_ALL, FRAMES)).astype(jnp.int32),
        "upstream": scatter_about(key_of[2], (CLIPS_ALL, FRAMES, POS, D), 1.0, 6.0, ((0, 8), (1, 64))),
        "out_weight": scatter_about(key_of[3], (INNER, D), INNER ** -0.5, 0.25, ((0, 8),)),
    }


def clip_pass(running, inputs, weight_all):
    packed, segment_row, upstream_clip = inputs
    inner = HEADS * HEAD_DIM
    factor = 1.0 / math.sqrt(HEAD_DIM)
    head_split = packed.reshape(FRAMES, POS, 3, HEADS, HEAD_DIM)
    queries = head_split[:, :, 0].astype(jnp.float32)
    key_part = head_split[:, :, 1].astype(jnp.float32)
    value_part = head_split[:, :, 2].astype(jnp.float32)
    scores = jnp.einsum('fphd,gphd->phfg', queries, key_part) * factor
    allowed = segment_row[:, None] == segment_row[None, :]
    scores = jnp.where(allowed, scores, jnp.float32(-1e+30))
    row_peak = lax.optimization_barrier(jnp.max(scores, axis=-1, keepdims=True))
    exponent = jnp.exp(scores - row_peak)
    attend = exponent / lax.optimization_barrier(jnp.sum(exponent, axis=-1, keepdims=True))
    attend_low = attend.astype(jnp.bfloat16)
    mixed = jnp.einsum('phfg,gphd->fphd', attend_low.astype(jnp.float32), value_part).astype(jnp.bfloat16)
    mixed_flat = mixed.reshape(FRAMES * POS, inner)
    upstream_flat = upstream_clip.reshape(FRAMES * POS, D)
    output = jnp.dot(mixed_flat, weight_all, preferred_element_type=jnp.float32).astype(jnp.bfloat16)
    mixed_grad = jnp.dot(upstream_flat, weight_all.T, preferred_element_type=jnp.float32).astype(jnp.bfloat16)
    partial_value = jnp.dot(mixed_flat.T, upstream_flat, preferred_element_type=jnp.float32)
    grad_heads = mixed_grad.reshape(FRAMES, POS, HEADS, HEAD_DIM).astype(jnp.float32)
    attend_grad = jnp.einsum('fphd,gphd->phfg', grad_heads, value_part)
    row_dot = lax.optimization_barrier(jnp.sum(attend * attend_grad, axis=-1, keepdims=True))
    score_grad = (attend * (attend_grad - row_dot)).astype(jnp.bfloat16).astype(jnp.float32)
    query_grad = (jnp.einsum('phfg,gphd->fphd', score_grad, key_part) * factor).astype(jnp.bfloat16)
    key_grad = (jnp.einsum('phfg,fphd->gphd', score_grad, queries) * factor).astype(jnp.bfloat16)
    value_grad = jnp.einsum('phfg,fphd->gphd', attend_low.astype(jnp.float32), grad_heads).astype(jnp.bfloat16)
    qkv_grad = jnp.stack([query_grad, key_grad, value_grad], axis=2).reshape(FRAMES, POS, 3 * inner)
    return (running + partial_value, (output.reshape(FRAMES, POS, D), qkv_grad))

def reference(qkv, segment_ids, upstream, out_weight):
    start = jnp.zeros((HEADS * HEAD_DIM, D), jnp.float32)

    def step_fn(running, inputs):
        return clip_pass(running, inputs, out_weight)
    summed, (output, qkv_grad) = lax.scan(step_fn, start, (qkv, segment_ids, upstream))
    weight_grad = summed / math.sqrt(TOKENS_ALL)
    return (output, qkv_grad, weight_grad)
```

```python
import math

import jax
import jax.numpy as jnp
from jax import lax
from jax.experimental import pallas as pl
from jax.experimental.pallas import tpu as pltpu
from jax.sharding import PartitionSpec as P

HEAD_DIM = 72
HEADS = 8
NX, NY, NZ = 4, 8, 8
MESH = pl.DeviceIdType.MESH
BF, F32 = jnp.bfloat16, jnp.float32


def place():
    dp, seq = lax.axis_index("dp"), lax.axis_index("seq")
    zh, core = dp // 2, dp % 2
    zl, y, x = seq // 32, (seq // 4) % 8, seq % 4
    return zh, core, zl, y, x


def device(zh, core, zl, y, x):
    return (zh * 2 + core, zl * 32 + y * 4 + x)


def peers():
    zh, core, zl, y, x = place()

    def at_core():
        return device(zh, 1 - core, zl, y, x)

    def at_x(r):
        return device(zh, core, zl, y, (x + r) % NX)

    def at_y(r):
        return device(zh, core, zl, (y + r) % NY, x)

    def at_z(r):
        z = (zh * 2 + zl + r) % NZ
        return device(z // 2, core, z % 2, y, x)

    def at_plane(r):
        return device(zh, core, zl, (y + r // NX) % NY, (x + r % NX) % NX)

    return at_core, at_x, at_y, at_z, at_plane


def weight_kernel(
    mixed_ref, up_ref, out_ref,
    own0, snd0, rcv0, snd1, rcv1, own1, snd2, rcv2, own2, snd3, rcv3, snd4, rcv4,
    s0, r0, s1, r1, s2, r2, s3, r3, s4, r4,
):
    zh, core, zl, y, x = place()
    at_core, at_x, at_y, at_z, at_plane = peers()

    barrier = pltpu.get_barrier_semaphore()
    pl.semaphore_signal(barrier, inc=1, device_id=at_core(), device_id_type=MESH)

    @pl.loop(1, NZ)
    def _(r):
        pl.semaphore_signal(barrier, inc=1, device_id=at_z(r), device_id_type=MESH)

    @pl.loop(1, NX * NY)
    def _(r):
        pl.semaphore_signal(barrier, inc=1, device_id=at_plane(r), device_id_type=MESH)

    def units(head, dst):
        rows = mixed_ref[head]
        for g in range(9):
            part = jnp.dot(
                rows, up_ref[:, g * 128:(g + 1) * 128], preferred_element_type=F32
            )
            yield g, part

    @pl.loop(0, 4)
    def _(h):
        for g, part in units(2 * h + 1 - core, snd0):
            for rb in range(9):
                u = rb * 9 + g
                snd0[u // 24, (u % 24) // 3, h, u % 3] = part[rb * 8:rb * 8 + 8].astype(BF)
        for u in range(81, 96):
            snd0[u // 24, (u % 24) // 3, h, u % 3] = jnp.zeros((8, 128), BF)

    pl.semaphore_wait(barrier, 1 + (NZ - 1) + (NX * NY - 1))

    copy0 = pltpu.make_async_remote_copy(
        src_ref=snd0, dst_ref=rcv0, send_sem=s0, recv_sem=r0,
        device_id=at_core(), device_id_type=MESH,
    )
    copy0.start()

    @pl.loop(0, 4)
    def _(h):
        for g, part in units(2 * h + core, own0):
            for rb in range(9):
                u = rb * 9 + g
                own0[u // 24, (u % 24) // 3, h, u % 3] = part[rb * 8:rb * 8 + 8]
        for u in range(81, 96):
            own0[u // 24, (u % 24) // 3, h, u % 3] = jnp.zeros((8, 128), F32)

    copy0.wait()

    def copy1(r):
        return pltpu.make_async_remote_copy(
            src_ref=snd1.at[r - 1], dst_ref=rcv1.at[r - 1],
            send_sem=s1.at[r - 1], recv_sem=r1.at[r - 1],
            device_id=at_x(r), device_id_type=MESH,
        )

    for r in (2, 1, 3):
        to = (x + r) % NX
        snd1[r - 1] = (own0[to] + rcv0[to].astype(F32)).astype(BF)
        copy1(r).start()
    own1[...] = own0[x] + rcv0[x].astype(F32)
    for r in (1, 3, 2):
        copy1(r).wait()
    own1[...] = (own1[...] + rcv1[0].astype(F32)) + (rcv1[1].astype(F32) + rcv1[2].astype(F32))

    def copy2(r):
        return pltpu.make_async_remote_copy(
            src_ref=snd2.at[r - 1], dst_ref=rcv2.at[r - 1],
            send_sem=s2.at[r - 1], recv_sem=r2.at[r - 1],
            device_id=at_y(r), device_id_type=MESH,
        )

    for r in (4, 3, 5, 2, 6, 1, 7):
        snd2[r - 1] = own1[(y + r) % NY].astype(BF)
        copy2(r).start()
    for r in (1, 7, 2, 6, 3, 5, 4):
        copy2(r).wait()
    total = own1[y]
    for r in range(NY - 1):
        total = total + rcv2[r].astype(F32)
    own2[...] = total

    def copy3(r):
        return pltpu.make_async_remote_copy(
            src_ref=snd3.at[r - 1], dst_ref=rcv3.at[r - 1],
            send_sem=s3.at[r - 1], recv_sem=r3.at[r - 1],
            device_id=at_z(r), device_id_type=MESH,
        )

    for r in (4, 3, 5, 2, 6, 1, 7):
        z = (zh * 2 + zl + r) % NZ
        snd3[r - 1] = own2[z // 2].astype(BF)
        copy3(r).start()
    for r in (1, 7, 2, 6, 3, 5, 4):
        copy3(r).wait()
    total = own2[zh]
    for r in range(NZ - 1):
        total = total + rcv3[r].astype(F32)
    snd4[...] = (total * (1.0 / 256.0)).astype(BF)

    me = x * NY + y

    def copy4(r):
        return pltpu.make_async_remote_copy(
            src_ref=snd4, dst_ref=rcv4.at[me],
            send_sem=s4, recv_sem=r4,
            device_id=at_plane(r), device_id_type=MESH,
        )

    @pl.loop(1, NX * NY)
    def _(r):
        copy4(r).start()

    keep = pltpu.make_async_copy(snd4, rcv4.at[me], r4)
    keep.start()
    pltpu.make_async_copy(rcv4, rcv4, r4).wait()
    sent = rcv4.at[pl.ds(0, NX * NY - 1)]
    pltpu.make_async_copy(sent, sent, s4).wait()
    for u in range(81):
        rb, g = u // 9, u % 9
        out_ref[rb * 8:rb * 8 + 8, g * 128:(g + 1) * 128] = rcv4[u // 3, u % 3].astype(F32)


def weight_sum(mixed_t, up):
    unit = (8, 128)
    vm = pltpu.VMEM
    dma = pltpu.SemaphoreType.DMA
    return pl.pallas_call(
        weight_kernel,
        out_shape=jax.ShapeDtypeStruct((HEAD_DIM, up.shape[1]), F32),
        in_specs=[pl.BlockSpec(memory_space=pltpu.VMEM)] * 2,
        out_specs=pl.BlockSpec(memory_space=pltpu.VMEM),
        scratch_shapes=[
            vm((4, 8, 4, 3) + unit, F32),
            vm((4, 8, 4, 3) + unit, BF),
            vm((4, 8, 4, 3) + unit, BF),
            vm((3, 8, 4, 3) + unit, BF),
            vm((3, 8, 4, 3) + unit, BF),
            vm((8, 4, 3) + unit, F32),
            vm((7, 4, 3) + unit, BF),
            vm((7, 4, 3) + unit, BF),
            vm((4, 3) + unit, F32),
            vm((7, 3) + unit, BF),
            vm((7, 3) + unit, BF),
            vm((3,) + unit, BF),
            vm((32, 3) + unit, BF),
            dma, dma,
            dma((3,)), dma((3,)),
            dma((7,)), dma((7,)),
            dma((7,)), dma((7,)),
            dma, dma,
        ],
        compiler_params=pltpu.CompilerParams(collective_id=1, has_side_effects=True),
        name="weight_sum",
    )(mixed_t, up)


def attend_all(stacked, grad_in, allowed, factor):
    frame_count, pos_here, _ = stacked.shape
    split = stacked.reshape(frame_count, pos_here, 3, HEADS, HEAD_DIM)
    queries, keys, values = split[:, :, 0], split[:, :, 1], split[:, :, 2]
    scores = jnp.einsum("fphd,gphd->phfg", queries, keys, preferred_element_type=F32) * factor
    scores = jnp.where(allowed, scores, F32(-1e30))
    exponent = jnp.exp(scores - jnp.max(scores, axis=-1, keepdims=True))
    attend = exponent / jnp.sum(exponent, axis=-1, keepdims=True)
    low = attend.astype(BF)
    mixed = jnp.einsum("phfg,gphd->fphd", low, values, preferred_element_type=F32).astype(BF)
    grad = grad_in.reshape(frame_count, pos_here, HEADS, HEAD_DIM)
    attend_grad = jnp.einsum("fphd,gphd->phfg", grad, values, preferred_element_type=F32)
    row_dot = jnp.sum(attend * attend_grad, axis=-1, keepdims=True)
    score_grad = (attend * (attend_grad - row_dot)).astype(BF)
    query_grad = (
        jnp.einsum("phfg,gphd->fphd", score_grad, keys, preferred_element_type=F32) * factor
    ).astype(BF)
    key_grad = (
        jnp.einsum("phfg,fphd->gphd", score_grad, queries, preferred_element_type=F32) * factor
    ).astype(BF)
    value_grad = jnp.einsum("phfg,fphd->gphd", low, grad, preferred_element_type=F32).astype(BF)
    packed = jnp.stack([query_grad, key_grad, value_grad], axis=2)
    return mixed, packed.reshape(frame_count, pos_here, 3 * HEADS * HEAD_DIM)


def on_device(qkv, segment_ids, upstream, out_weight):
    _, _, positions, packed = qkv.shape
    inner = HEADS * HEAD_DIM
    factor = 1.0 / math.sqrt(HEAD_DIM)
    full_weight = lax.all_gather(out_weight, "dp", axis=0, tiled=True)
    width = full_weight.shape[1]
    frames = lax.axis_size("seq")
    pos_here = positions // frames
    allowed = (segment_ids[0, :, None] == segment_ids[0, None, :])[None, None]

    both = jnp.concatenate([qkv, upstream], axis=-1).reshape(frames, pos_here, packed + width)
    both = lax.all_to_all(both, "seq", split_axis=0, concat_axis=0, tiled=True)
    stacked, up = both[..., :packed], both[..., packed:].reshape(frames * pos_here, width)

    grad_in = lax.dot_general(
        up, full_weight, (((1,), (1,)), ((), ())), preferred_element_type=F32
    ).astype(BF)
    mixed, packed_grad = attend_all(stacked, grad_in, allowed, factor)
    mixed_flat = mixed.reshape(frames * pos_here, inner)
    weight_grad = weight_sum(mixed_flat.T.reshape(HEADS, HEAD_DIM, -1), up)

    back = jnp.concatenate([packed_grad, mixed.reshape(frames, pos_here, inner)], axis=-1)
    back = lax.all_to_all(back, "seq", split_axis=0, concat_axis=0, tiled=True)
    back = back.reshape(positions, packed + inner)
    qkv_grad = back[:, :packed].reshape(qkv.shape)
    output = jnp.dot(back[:, packed:], full_weight, preferred_element_type=F32).astype(BF)
    return (output.reshape(upstream.shape), qkv_grad, weight_grad)


def solution(mesh):
    in_specs = (
        P("dp", "seq", None, None),
        P("dp", None),
        P("dp", "seq", None, None),
        P("dp", None),
    )
    out_specs = (P("dp", "seq", None, None), P("dp", "seq", None, None), P("dp", None))
    return jax.shard_map(
        on_device, mesh=mesh, in_specs=in_specs, out_specs=out_specs, check_vma=False
    )
```

```python
import math

import jax
import jax.numpy as jnp
from jax import lax
from jax.experimental import pallas as pl
from jax.experimental.pallas import tpu as pltpu
from jax.sharding import PartitionSpec as P

HEAD_DIM = 72
HEADS = 8
NX, NY, NZ = 4, 8, 8
MESH = pl.DeviceIdType.MESH
BF, F32 = jnp.bfloat16, jnp.float32


def place():
    dp, seq = lax.axis_index("dp"), lax.axis_index("seq")
    zh, core = dp // 2, dp % 2
    zl, y, x = seq // 32, (seq // 4) % 8, seq % 4
    return zh, core, zl, y, x


def device(zh, core, zl, y, x):
    return (zh * 2 + core, zl * 32 + y * 4 + x)


def peers():
    zh, core, zl, y, x = place()

    def at_core():
        return device(zh, 1 - core, zl, y, x)

    def at_x(r):
        return device(zh, core, zl, y, (x + r) % NX)

    def at_y(r):
        return device(zh, core, zl, (y + r) % NY, x)

    def at_z(r):
        z = (zh * 2 + zl + r) % NZ
        return device(z // 2, core, z % 2, y, x)

    def at_plane(r):
        return device(zh, core, zl, (y + r // NX) % NY, (x + r % NX) % NX)

    def at_seq(r):
        return device(zh, core, (zl + r // 32) % 2, (y + r // NX) % NY, (x + r % NX) % NX)

    return at_core, at_x, at_y, at_z, at_plane, at_seq


def exchange(src, dst, send_sem, recv_sem, keep_sem):
    _, _, _, _, _, at_seq = peers()
    me = lax.axis_index("seq")

    def start(r):
        to = at_seq(r)
        pltpu.make_async_remote_copy(
            src_ref=src.at[to[1]], dst_ref=dst.at[me], send_sem=send_sem, recv_sem=recv_sem,
            device_id=to, device_id_type=MESH,
        ).start()

    def keep():
        return pltpu.make_async_copy(src.at[me], dst.at[me], keep_sem)

    def finish():
        keep().wait()
        others = dst.at[pl.ds(0, NX * NY * 2 - 1)]
        pltpu.make_async_copy(others, others, recv_sem).wait()
        pltpu.make_async_copy(others, others, send_sem).wait()

    return start, keep, finish


def greet(barrier):
    at_core, _, _, at_z, _, at_seq = peers()
    pl.semaphore_signal(barrier, inc=1, device_id=at_core(), device_id_type=MESH)

    @pl.loop(1, NZ)
    def _(r):
        pl.semaphore_signal(barrier, inc=1, device_id=at_z(r), device_id_type=MESH)

    @pl.loop(1, NX * NY * 2)
    def _(r):
        pl.semaphore_signal(barrier, inc=1, device_id=at_seq(r), device_id_type=MESH)


GREETED = 1 + (NZ - 1) + (NX * NY * 2 - 1)


def enter_kernel(
    qkv_ref, up_ref, w_ref, qkv_out, up_out, w_out,
    qs, qr, qk, us, ur, uk, wk, os, orr, zs, zr, xs, xr, cs, cr, ds, dr,
):
    zh, core, zl, y, x = place()
    dp = zh * 2 + core
    at_core = peers()[0]
    barrier = pltpu.get_barrier_semaphore()
    greet(barrier)
    q_start, q_keep, q_finish = exchange(qkv_ref, qkv_out, qs, qr, qk)
    u_start, u_keep, u_finish = exchange(up_ref, up_out, us, ur, uk)
    q_keep().start()
    u_keep().start()
    w_keep = pltpu.make_async_copy(w_ref, w_out.at[dp], wk)
    w_keep.start()
    pl.semaphore_wait(barrier, GREETED)

    def remote(src, dst, ss, rs, to):
        return pltpu.make_async_remote_copy(
            src_ref=src, dst_ref=dst, send_sem=ss, recv_sem=rs,
            device_id=to, device_id_type=MESH,
        )

    def over_z(r, part):
        to = device((zh + r) % 4, core, zl, y, x)
        return remote(w_ref.at[part], w_out.at[dp, part], zs.at[r - 1], zr.at[r - 1], to)

    def landed(r, part, sem):
        ref = w_out.at[((zh + 4 - r) % 4) * 2 + core, part]
        pltpu.make_async_copy(ref, ref, sem).wait()
        return ref

    def landed_core(r, part, sem):
        ref = w_out.at[((zh + 4 - r) % 4) * 2 + 1 - core, part]
        pltpu.make_async_copy(ref, ref, sem).wait()

    halves = (pl.ds(0, 5), pl.ds(5, 4))
    own_core = remote(w_ref, w_out.at[dp], os, orr, at_core())
    for half in (0, 1):
        @pl.when(x % 2 == half)
        def _(half=half):
            for r in (2, 1, 3):
                over_z(r, halves[half]).start()

    own_core.start()

    @pl.loop(1, NX * NY * 2)
    def _(r):
        q_start(NX * NY * 2 - r)

    @pl.loop(1, NX * NY * 2)
    def _(r):
        u_start(NX * NY * 2 - r)

    across = device(zh, core, zl, y, x + 1 - 2 * (x % 2))
    for half in (0, 1):
        @pl.when(x % 2 == half)
        def _(half=half):
            mine, other = halves[half], halves[1 - half]
            for r in (1, 3, 2):
                ref = landed(r, mine, zr.at[r - 1])
                remote(ref, ref, xs.at[r - 1], xr.at[r - 1], across).start()
                remote(ref, ref, cs.at[r - 1], cr.at[r - 1], at_core()).start()
            for r in (1, 3, 2):
                ref = landed(r, other, xr.at[r - 1])
                remote(ref, ref, ds.at[r - 1], dr.at[r - 1], at_core()).start()
            for r in (1, 3, 2):
                over_z(r, mine).wait_send()
                landed(r, mine, xs.at[r - 1])
                landed(r, mine, cs.at[r - 1])
                landed(r, other, ds.at[r - 1])
                landed_core(r, mine, cr.at[r - 1])
                landed_core(r, other, dr.at[r - 1])

    own_core.wait()
    w_keep.wait()
    q_finish()
    u_finish()


def enter(qkv, up, weight):
    dma = pltpu.SemaphoreType.DMA
    spec = pl.BlockSpec(memory_space=pltpu.VMEM)
    return pl.pallas_call(
        enter_kernel,
        out_shape=[
            jax.ShapeDtypeStruct(qkv.shape, BF),
            jax.ShapeDtypeStruct(up.shape, BF),
            jax.ShapeDtypeStruct((HEADS,) + weight.shape, BF),
        ],
        in_specs=[spec] * 3,
        out_specs=[spec] * 3,
        scratch_shapes=[dma] * 9 + [dma((3,))] * 8,
        compiler_params=pltpu.CompilerParams(collective_id=0, has_side_effects=True),
        name="enter",
    )(qkv, up, weight)


def leave_kernel(
    grad_ref, back_ref, mixed_ref, up_ref, grad_out, back_out, out_ref,
    gs, gr, gk, bs, br, bk,
    own0, snd0, rcv0, snd1, rcv1, own1, snd2, rcv2, own2, snd3, rcv3, snd4, rcv4,
    s0, r0, s1, r1, s2, r2, s3, r3, s4, r4,
):
    zh, core, zl, y, x = place()
    at_core, at_x, at_y, at_z, at_plane, _ = peers()

    barrier = pltpu.get_barrier_semaphore()
    greet(barrier)
    g_start, g_keep, g_finish = exchange(grad_ref, grad_out, gs, gr, gk)
    b_start, b_keep, b_finish = exchange(back_ref, back_out, bs, br, bk)
    g_keep().start()
    b_keep().start()

    def units(head, dst):
        rows = mixed_ref[head]
        for g in range(9):
            part = jnp.dot(
                rows, up_ref[:, g * 128:(g + 1) * 128], preferred_element_type=F32
            )
            yield g, part

    @pl.loop(0, 4)
    def _(h):
        for g, part in units(2 * h + 1 - core, snd0):
            for rb in range(9):
                u = rb * 9 + g
                snd0[u // 24, (u % 24) // 3, h, u % 3] = part[rb * 8:rb * 8 + 8].astype(BF)
        for u in range(81, 96):
            snd0[u // 24, (u % 24) // 3, h, u % 3] = jnp.zeros((8, 128), BF)

    pl.semaphore_wait(barrier, GREETED)

    copy0 = pltpu.make_async_remote_copy(
        src_ref=snd0, dst_ref=rcv0, send_sem=s0, recv_sem=r0,
        device_id=at_core(), device_id_type=MESH,
    )
    copy0.start()

    @pl.loop(1, NX * NY * 2)
    def _(r):
        g_start(NX * NY * 2 - r)

    @pl.loop(1, NX * NY * 2)
    def _(r):
        b_start(NX * NY * 2 - r)

    @pl.loop(0, 4)
    def _(h):
        for g, part in units(2 * h + core, own0):
            for rb in range(9):
                u = rb * 9 + g
                own0[u // 24, (u % 24) // 3, h, u % 3] = part[rb * 8:rb * 8 + 8]
        for u in range(81, 96):
            own0[u // 24, (u % 24) // 3, h, u % 3] = jnp.zeros((8, 128), F32)

    copy0.wait()

    def copy1(r):
        return pltpu.make_async_remote_copy(
            src_ref=snd1.at[r - 1], dst_ref=rcv1.at[r - 1],
            send_sem=s1.at[r - 1], recv_sem=r1.at[r - 1],
            device_id=at_x(r), device_id_type=MESH,
        )

    for r in (2, 1, 3):
        to = (x + r) % NX
        snd1[r - 1] = (own0[to] + rcv0[to].astype(F32)).astype(BF)
        copy1(r).start()
    own1[...] = own0[x] + rcv0[x].astype(F32)
    for r in (1, 3, 2):
        copy1(r).wait()
    own1[...] = (own1[...] + rcv1[0].astype(F32)) + (rcv1[1].astype(F32) + rcv1[2].astype(F32))

    def copy2(r):
        return pltpu.make_async_remote_copy(
            src_ref=snd2.at[r - 1], dst_ref=rcv2.at[r - 1],
            send_sem=s2.at[r - 1], recv_sem=r2.at[r - 1],
            device_id=at_y(r), device_id_type=MESH,
        )

    for r in (4, 3, 5, 2, 6, 1, 7):
        snd2[r - 1] = own1[(y + r) % NY].astype(BF)
        copy2(r).start()
    for r in (1, 7, 2, 6, 3, 5, 4):
        copy2(r).wait()
    total = own1[y]
    for r in range(NY - 1):
        total = total + rcv2[r].astype(F32)
    own2[...] = total

    def copy3(r):
        return pltpu.make_async_remote_copy(
            src_ref=snd3.at[r - 1], dst_ref=rcv3.at[r - 1],
            send_sem=s3.at[r - 1], recv_sem=r3.at[r - 1],
            device_id=at_z(r), device_id_type=MESH,
        )

    for r in (4, 3, 5, 2, 6, 1, 7):
        z = (zh * 2 + zl + r) % NZ
        snd3[r - 1] = own2[z // 2].astype(BF)
        copy3(r).start()
    for r in (1, 7, 2, 6, 3, 5, 4):
        copy3(r).wait()
    total = own2[zh]
    for r in range(NZ - 1):
        total = total + rcv3[r].astype(F32)
    snd4[...] = (total * (1.0 / 256.0)).astype(BF)

    me = x * NY + y

    def copy4(r):
        return pltpu.make_async_remote_copy(
            src_ref=snd4, dst_ref=rcv4.at[me],
            send_sem=s4, recv_sem=r4,
            device_id=at_plane(r), device_id_type=MESH,
        )

    @pl.loop(1, NX * NY)
    def _(r):
        copy4(r).start()

    keep = pltpu.make_async_copy(snd4, rcv4.at[me], r4)
    keep.start()
    pltpu.make_async_copy(rcv4, rcv4, r4).wait()
    sent = rcv4.at[pl.ds(0, NX * NY - 1)]
    pltpu.make_async_copy(sent, sent, s4).wait()
    for u in range(81):
        rb, g = u // 9, u % 9
        out_ref[rb * 8:rb * 8 + 8, g * 128:(g + 1) * 128] = rcv4[u // 3, u % 3].astype(F32)
    g_finish()
    b_finish()


def leave(grad, back, mixed_t, up):
    unit = (8, 128)
    vm = pltpu.VMEM
    dma = pltpu.SemaphoreType.DMA
    return pl.pallas_call(
        leave_kernel,
        out_shape=[
            jax.ShapeDtypeStruct(grad.shape, BF),
            jax.ShapeDtypeStruct(back.shape, BF),
            jax.ShapeDtypeStruct((HEAD_DIM, up.shape[1]), F32),
        ],
        in_specs=[pl.BlockSpec(memory_space=pltpu.VMEM)] * 4,
        out_specs=[pl.BlockSpec(memory_space=pltpu.VMEM)] * 3,
        scratch_shapes=[dma] * 6 + [
            vm((4, 8, 4, 3) + unit, F32),
            vm((4, 8, 4, 3) + unit, BF),
            vm((4, 8, 4, 3) + unit, BF),
            vm((3, 8, 4, 3) + unit, BF),
            vm((3, 8, 4, 3) + unit, BF),
            vm((8, 4, 3) + unit, F32),
            vm((7, 4, 3) + unit, BF),
            vm((7, 4, 3) + unit, BF),
            vm((4, 3) + unit, F32),
            vm((7, 3) + unit, BF),
            vm((7, 3) + unit, BF),
            vm((3,) + unit, BF),
            vm((32, 3) + unit, BF),
            dma, dma,
            dma((3,)), dma((3,)),
            dma((7,)), dma((7,)),
            dma((7,)), dma((7,)),
            dma, dma,
        ],
        compiler_params=pltpu.CompilerParams(collective_id=1, has_side_effects=True),
        name="leave",
    )(grad, back, mixed_t, up)


def attend_all(stacked, grad_in, allowed, factor):
    frame_count, pos_here, _ = stacked.shape
    split = stacked.reshape(frame_count, pos_here, 3, HEADS, HEAD_DIM)
    queries, keys, values = split[:, :, 0], split[:, :, 1], split[:, :, 2]
    scores = jnp.einsum("fphd,gphd->phfg", queries, keys, preferred_element_type=F32) * factor
    scores = jnp.where(allowed, scores, F32(-1e30))
    exponent = jnp.exp(scores - jnp.max(scores, axis=-1, keepdims=True))
    attend = exponent / jnp.sum(exponent, axis=-1, keepdims=True)
    low = attend.astype(BF)
    mixed = jnp.einsum("phfg,gphd->fphd", low, values, preferred_element_type=F32).astype(BF)
    grad = grad_in.reshape(frame_count, pos_here, HEADS, HEAD_DIM)
    attend_grad = jnp.einsum("fphd,gphd->phfg", grad, values, preferred_element_type=F32)
    row_dot = jnp.sum(attend * attend_grad, axis=-1, keepdims=True)
    score_grad = (attend * (attend_grad - row_dot)).astype(BF)
    query_grad = (
        jnp.einsum("phfg,gphd->fphd", score_grad, keys, preferred_element_type=F32) * factor
    ).astype(BF)
    key_grad = (
        jnp.einsum("phfg,fphd->gphd", score_grad, queries, preferred_element_type=F32) * factor
    ).astype(BF)
    value_grad = jnp.einsum("phfg,fphd->gphd", low, grad, preferred_element_type=F32).astype(BF)
    packed = jnp.stack([query_grad, key_grad, value_grad], axis=2)
    return mixed, packed.reshape(frame_count, pos_here, 3 * HEADS * HEAD_DIM)


def on_device(qkv, segment_ids, upstream, out_weight):
    _, _, positions, packed = qkv.shape
    inner = HEADS * HEAD_DIM
    factor = 1.0 / math.sqrt(HEAD_DIM)
    width = out_weight.shape[1]
    frames = lax.axis_size("seq")
    pos_here = positions // frames
    allowed = (segment_ids[0, :, None] == segment_ids[0, None, :])[None, None]

    stacked, up, full_weight = enter(
        qkv.reshape(frames, pos_here, packed),
        upstream.reshape(frames, pos_here, width),
        out_weight.reshape(HEAD_DIM // 8, 8, width),
    )
    full_weight = full_weight.reshape(inner, width)
    up = up.reshape(frames * pos_here, width)

    grad_in = lax.dot_general(
        up, full_weight, (((1,), (1,)), ((), ())), preferred_element_type=F32
    ).astype(BF)
    mixed, packed_grad = attend_all(stacked, grad_in, allowed, factor)
    mixed_t = mixed.reshape(frames * pos_here, inner).T.reshape(HEADS, HEAD_DIM, -1)
    back = mixed.reshape(frames, pos_here, inner)
    qkv_grad, back, weight_grad = leave(packed_grad, back, mixed_t, up)
    output = jnp.dot(
        back.reshape(positions, inner), full_weight, preferred_element_type=F32
    ).astype(BF)
    return (output.reshape(upstream.shape), qkv_grad.reshape(qkv.shape), weight_grad)


def solution(mesh):
    in_specs = (
        P("dp", "seq", None, None),
        P("dp", None),
        P("dp", "seq", None, None),
        P("dp", None),
    )
    out_specs = (P("dp", "seq", None, None), P("dp", "seq", None, None), P("dp", None))
    return jax.shard_map(
        on_device, mesh=mesh, in_specs=in_specs, out_specs=out_specs, check_vma=False
    )
```

```python
import math

import jax
import jax.numpy as jnp
from jax import lax
from jax.experimental import pallas as pl
from jax.experimental.pallas import tpu as pltpu
from jax.sharding import PartitionSpec as P

HEAD_DIM = 72
HEADS = 8
NX, NY, NZ = 4, 8, 8
MESH = pl.DeviceIdType.MESH
BF, F32 = jnp.bfloat16, jnp.float32


def place():
    dp, seq = lax.axis_index("dp"), lax.axis_index("seq")
    zh, core = dp // 2, dp % 2
    zl, y, x = seq // 32, (seq // 4) % 8, seq % 4
    return zh, core, zl, y, x


def device(zh, core, zl, y, x):
    return (zh * 2 + core, zl * 32 + y * 4 + x)


def peers():
    zh, core, zl, y, x = place()

    def at_core():
        return device(zh, 1 - core, zl, y, x)

    def at_x(r):
        return device(zh, core, zl, y, (x + r) % NX)

    def at_y(r):
        return device(zh, core, zl, (y + r) % NY, x)

    def at_z(r):
        z = (zh * 2 + zl + r) % NZ
        return device(z // 2, core, z % 2, y, x)

    def at_plane(r):
        return device(zh, core, zl, (y + r // NX) % NY, (x + r % NX) % NX)

    def at_seq(k):
        i, c = k % 8, k // 8
        dy = 4 + (i // 2) * (1 - 2 * (i % 2)) - i % 2
        return device(zh, core, (zl + c // 4 + i) % 2, (y + dy) % NY, (x + c + i) % NX)

    return at_core, at_x, at_y, at_z, at_plane, at_seq


def exchange(src, dst, send_sem, recv_sem, keep_sem):
    _, _, _, _, _, at_seq = peers()
    me = lax.axis_index("seq")

    def start(r):
        to = at_seq(r)
        pltpu.make_async_remote_copy(
            src_ref=src.at[to[1]], dst_ref=dst.at[me], send_sem=send_sem, recv_sem=recv_sem,
            device_id=to, device_id_type=MESH,
        ).start()

    def keep():
        return pltpu.make_async_copy(src.at[me], dst.at[me], keep_sem)

    def finish():
        keep().wait()
        others = dst.at[pl.ds(0, NX * NY * 2 - 1)]
        pltpu.make_async_copy(others, others, recv_sem).wait()
        pltpu.make_async_copy(others, others, send_sem).wait()

    return start, keep, finish


def greet(barrier):
    at_core, _, _, at_z, _, at_seq = peers()
    pl.semaphore_signal(barrier, inc=1, device_id=at_core(), device_id_type=MESH)

    @pl.loop(1, NZ)
    def _(r):
        pl.semaphore_signal(barrier, inc=1, device_id=at_z(r), device_id_type=MESH)

    @pl.loop(48, 48 + 63)
    def _(k):
        pl.semaphore_signal(barrier, inc=1, device_id=at_seq(k % 64), device_id_type=MESH)


GREETED = 1 + (NZ - 1) + (NX * NY * 2 - 1)


def enter_kernel(
    qkv_ref, up_ref, w_ref, qkv_out, up_out, w_out,
    qs, qr, qk, us, ur, uk, wk, os, orr, zs, zr, xs, xr, cs, cr, ds, dr,
):
    zh, core, zl, y, x = place()
    dp = zh * 2 + core
    at_core = peers()[0]
    barrier = pltpu.get_barrier_semaphore()
    greet(barrier)
    q_start, q_keep, q_finish = exchange(qkv_ref, qkv_out, qs, qr, qk)
    u_start, u_keep, u_finish = exchange(up_ref, up_out, us, ur, uk)
    q_keep().start()
    u_keep().start()
    w_keep = pltpu.make_async_copy(w_ref, w_out.at[dp], wk)
    w_keep.start()
    pl.semaphore_wait(barrier, GREETED)

    def remote(src, dst, ss, rs, to):
        return pltpu.make_async_remote_copy(
            src_ref=src, dst_ref=dst, send_sem=ss, recv_sem=rs,
            device_id=to, device_id_type=MESH,
        )

    def over_z(r, part):
        to = device((zh + r) % 4, core, zl, y, x)
        return remote(w_ref.at[part], w_out.at[dp, part], zs.at[r - 1], zr.at[r - 1], to)

    def landed(r, part, sem):
        ref = w_out.at[((zh + 4 - r) % 4) * 2 + core, part]
        pltpu.make_async_copy(ref, ref, sem).wait()
        return ref

    def landed_core(r, part, sem):
        ref = w_out.at[((zh + 4 - r) % 4) * 2 + 1 - core, part]
        pltpu.make_async_copy(ref, ref, sem).wait()

    halves = (pl.ds(0, 5), pl.ds(5, 4))
    own_core = remote(w_ref, w_out.at[dp], os, orr, at_core())
    for half in (0, 1):
        @pl.when(x % 2 == half)
        def _(half=half):
            for r in (2, 1, 3):
                over_z(r, halves[half]).start()

    own_core.start()

    def send_in(low, high):
        @pl.loop(48 + low, 48 + high)
        def _(k):
            q_start(k % 64)
            u_start(k % 64)

    send_in(0, 63)
    across = device(zh, core, zl, y, x + 1 - 2 * (x % 2))
    for half in (0, 1):
        @pl.when(x % 2 == half)
        def _(half=half):
            mine, other = halves[half], halves[1 - half]
            for r in (1, 3, 2):
                ref = landed(r, mine, zr.at[r - 1])
                remote(ref, ref, xs.at[r - 1], xr.at[r - 1], across).start()
                remote(ref, ref, cs.at[r - 1], cr.at[r - 1], at_core()).start()

    for half in (0, 1):
        @pl.when(x % 2 == half)
        def _(half=half):
            mine, other = halves[half], halves[1 - half]
            for r in (1, 3, 2):
                ref = landed(r, other, xr.at[r - 1])
                remote(ref, ref, ds.at[r - 1], dr.at[r - 1], at_core()).start()
            for r in (1, 3, 2):
                over_z(r, mine).wait_send()
                landed(r, mine, xs.at[r - 1])
                landed(r, mine, cs.at[r - 1])
                landed(r, other, ds.at[r - 1])
                landed_core(r, mine, cr.at[r - 1])
                landed_core(r, other, dr.at[r - 1])

    own_core.wait()
    w_keep.wait()
    q_finish()
    u_finish()


def enter(qkv, up, weight):
    dma = pltpu.SemaphoreType.DMA
    spec = pl.BlockSpec(memory_space=pltpu.VMEM)
    return pl.pallas_call(
        enter_kernel,
        out_shape=[
            jax.ShapeDtypeStruct(qkv.shape, BF),
            jax.ShapeDtypeStruct(up.shape, BF),
            jax.ShapeDtypeStruct((HEADS,) + weight.shape, BF),
        ],
        in_specs=[spec] * 3,
        out_specs=[spec] * 3,
        scratch_shapes=[dma] * 9 + [dma((3,))] * 8,
        compiler_params=pltpu.CompilerParams(collective_id=0, has_side_effects=True),
        name="enter",
    )(qkv, up, weight)


def leave_kernel(
    grad_ref, back_ref, mixed_ref, up_ref, grad_out, back_out, out_ref,
    gs, gr, gk, bs, br, bk,
    own0, rows0, cols0, snd1, rcv1, own1, snd2, rcv2, own2, snd3, rcv3, snd4, rcv4,
    s0, r0, t0, q0, s1, r1, s2, r2, s3, r3, s4, r4,
):
    zh, core, zl, y, x = place()
    at_core, at_x, at_y, at_z, at_plane, _ = peers()

    barrier = pltpu.get_barrier_semaphore()
    greet(barrier)
    g_start, g_keep, g_finish = exchange(grad_ref, grad_out, gs, gr, gk)
    b_start, b_keep, b_finish = exchange(back_ref, back_out, bs, br, bk)
    g_keep().start()
    b_keep().start()

    def add(rows, cols, first):
        for g in range(9):
            part = jnp.dot(
                rows[...], cols[:, g * 128:(g + 1) * 128], preferred_element_type=F32
            )
            for h in range(4):
                for rb in range(9):
                    u, at = rb * 9 + g, h * HEAD_DIM + rb * 8
                    spot = (u // 24, (u % 24) // 3, h, u % 3)
                    unit = part[at:at + 8]
                    own0[spot] = unit if first else own0[spot] + unit

    add(mixed_ref.at[core], up_ref, True)
    for h in range(4):
        for u in range(81, 96):
            own0[u // 24, (u % 24) // 3, h, u % 3] = jnp.zeros((8, 128), F32)
    pl.semaphore_wait(barrier, GREETED)

    def to_core(src, dst, ss, rs):
        return pltpu.make_async_remote_copy(
            src_ref=src, dst_ref=dst, send_sem=ss, recv_sem=rs,
            device_id=at_core(), device_id_type=MESH,
        )

    trade = (
        to_core(mixed_ref.at[1 - core], rows0, s0, r0),
        to_core(up_ref, cols0, t0, q0),
    )
    for copy in trade:
        copy.start()

    def send_back(low, high):
        @pl.loop(48 + low, 48 + high)
        def _(k):
            g_start(k % 64)
            b_start(k % 64)

    for copy in trade:
        copy.wait()
    add(rows0, cols0, False)

    def copy1(r):
        return pltpu.make_async_remote_copy(
            src_ref=snd1.at[r - 1], dst_ref=rcv1.at[r - 1],
            send_sem=s1.at[r - 1], recv_sem=r1.at[r - 1],
            device_id=at_x(r), device_id_type=MESH,
        )

    for r in (2, 1, 3):
        to = (x + r) % NX
        snd1[r - 1] = own0[to].astype(BF)
        copy1(r).start()
    send_back(0, 32)
    own1[...] = own0[x]
    for r in (1, 3, 2):
        copy1(r).wait()
    own1[...] = (own1[...] + rcv1[0].astype(F32)) + (rcv1[1].astype(F32) + rcv1[2].astype(F32))

    def copy2(r):
        return pltpu.make_async_remote_copy(
            src_ref=snd2.at[r - 1], dst_ref=rcv2.at[r - 1],
            send_sem=s2.at[r - 1], recv_sem=r2.at[r - 1],
            device_id=at_y(r), device_id_type=MESH,
        )

    for r in (4, 3, 5, 2, 6, 1, 7):
        snd2[r - 1] = own1[(y + r) % NY].astype(BF)
        copy2(r).start()
    send_back(32, 48)
    for r in (1, 7, 2, 6, 3, 5, 4):
        copy2(r).wait()
    total = own1[y]
    for r in range(NY - 1):
        total = total + rcv2[r].astype(F32)
    own2[...] = total

    def copy3(r):
        return pltpu.make_async_remote_copy(
            src_ref=snd3.at[r - 1], dst_ref=rcv3.at[r - 1],
            send_sem=s3.at[r - 1], recv_sem=r3.at[r - 1],
            device_id=at_z(r), device_id_type=MESH,
        )

    for r in (4, 3, 5, 2, 6, 1, 7):
        z = (zh * 2 + zl + r) % NZ
        snd3[r - 1] = own2[z // 2].astype(BF)
        copy3(r).start()
    send_back(48, 63)
    for r in (1, 7, 2, 6, 3, 5, 4):
        copy3(r).wait()
    total = own2[zh]
    for r in range(NZ - 1):
        total = total + rcv3[r].astype(F32)
    snd4[...] = (total * (1.0 / 256.0)).astype(BF)

    me = x * NY + y

    def copy4(r):
        return pltpu.make_async_remote_copy(
            src_ref=snd4, dst_ref=rcv4.at[me],
            send_sem=s4, recv_sem=r4,
            device_id=at_plane(r), device_id_type=MESH,
        )

    @pl.loop(1, NX * NY)
    def _(r):
        copy4(r).start()

    keep = pltpu.make_async_copy(snd4, rcv4.at[me], r4)
    keep.start()
    pltpu.make_async_copy(rcv4, rcv4, r4).wait()
    sent = rcv4.at[pl.ds(0, NX * NY - 1)]
    pltpu.make_async_copy(sent, sent, s4).wait()
    result = pltpu.make_async_copy(rcv4, out_ref, s4)
    result.start()
    result.wait()
    g_finish()
    b_finish()


def leave(grad, back, mixed_t, up):
    unit = (8, 128)
    vm = pltpu.VMEM
    dma = pltpu.SemaphoreType.DMA
    return pl.pallas_call(
        leave_kernel,
        out_shape=[
            jax.ShapeDtypeStruct(grad.shape, BF),
            jax.ShapeDtypeStruct(back.shape, BF),
            jax.ShapeDtypeStruct((32, 3, 8, 128), BF),
        ],
        in_specs=[pl.BlockSpec(memory_space=pltpu.VMEM)] * 4,
        out_specs=[pl.BlockSpec(memory_space=pltpu.VMEM)] * 3,
        scratch_shapes=[dma] * 6 + [
            vm((4, 8, 4, 3) + unit, F32),
            vm((4 * HEAD_DIM, up.shape[0]), BF),
            vm(up.shape, BF),
            vm((3, 8, 4, 3) + unit, BF),
            vm((3, 8, 4, 3) + unit, BF),
            vm((8, 4, 3) + unit, F32),
            vm((7, 4, 3) + unit, BF),
            vm((7, 4, 3) + unit, BF),
            vm((4, 3) + unit, F32),
            vm((7, 3) + unit, BF),
            vm((7, 3) + unit, BF),
            vm((3,) + unit, BF),
            vm((32, 3) + unit, BF),
            dma, dma, dma, dma,
            dma((3,)), dma((3,)),
            dma((7,)), dma((7,)),
            dma((7,)), dma((7,)),
            dma, dma,
        ],
        compiler_params=pltpu.CompilerParams(collective_id=1, has_side_effects=True),
        name="leave",
    )(grad, back, mixed_t, up)


def attend_all(stacked, grad_in, allowed, factor):
    frame_count, pos_here, _ = stacked.shape
    split = stacked.reshape(frame_count, pos_here, 3, HEADS, HEAD_DIM)
    queries, keys, values = split[:, :, 0], split[:, :, 1], split[:, :, 2]
    scores = jnp.einsum("fphd,gphd->phfg", queries, keys, preferred_element_type=F32) * factor
    scores = jnp.where(allowed, scores, F32(-1e30))
    exponent = jnp.exp(scores - jnp.max(scores, axis=-1, keepdims=True))
    attend = exponent / jnp.sum(exponent, axis=-1, keepdims=True)
    low = attend.astype(BF)
    mixed = jnp.einsum("phfg,gphd->fphd", low, values, preferred_element_type=F32).astype(BF)
    grad = grad_in.reshape(frame_count, pos_here, HEADS, HEAD_DIM)
    attend_grad = jnp.einsum("fphd,gphd->phfg", grad, values, preferred_element_type=F32)
    row_dot = jnp.sum(attend * attend_grad, axis=-1, keepdims=True)
    score_grad = (attend * (attend_grad - row_dot)).astype(BF)
    query_grad = (
        jnp.einsum("phfg,gphd->fphd", score_grad, keys, preferred_element_type=F32) * factor
    ).astype(BF)
    key_grad = (
        jnp.einsum("phfg,fphd->gphd", score_grad, queries, preferred_element_type=F32) * factor
    ).astype(BF)
    value_grad = jnp.einsum("phfg,fphd->gphd", low, grad, preferred_element_type=F32).astype(BF)
    packed = jnp.stack([query_grad, key_grad, value_grad], axis=2)
    return mixed, packed.reshape(frame_count, pos_here, 3 * HEADS * HEAD_DIM)


def on_device(qkv, segment_ids, upstream, out_weight):
    _, _, positions, packed = qkv.shape
    inner = HEADS * HEAD_DIM
    factor = 1.0 / math.sqrt(HEAD_DIM)
    width = out_weight.shape[1]
    frames = lax.axis_size("seq")
    pos_here = positions // frames
    stacked, up, full_weight = enter(
        qkv.reshape(frames, pos_here, packed),
        upstream.reshape(frames, pos_here, width),
        out_weight.reshape(HEAD_DIM // 8, 8, width),
    )
    stacked, segment_ids = lax.optimization_barrier((stacked, segment_ids))
    allowed = (segment_ids[0, :, None] == segment_ids[0, None, :])[None, None]
    full_weight = full_weight.reshape(inner, width)
    up = up.reshape(frames * pos_here, width)

    grad_in = lax.dot_general(
        up, full_weight, (((1,), (1,)), ((), ())), preferred_element_type=F32
    ).astype(BF)
    mixed, packed_grad = attend_all(stacked, grad_in, allowed, factor)
    mixed_t = mixed.reshape(frames * pos_here, HEADS // 2, 2, HEAD_DIM)
    mixed_t = mixed_t.transpose(2, 1, 3, 0).reshape(2, inner // 2, frames * pos_here)
    back = mixed.reshape(frames, pos_here, inner)
    qkv_grad, back, units = leave(packed_grad, back, mixed_t, up)
    units = units.reshape(96, 8, 128)[:81].reshape(9, 9, 8, 128)
    weight_grad = units.transpose(0, 2, 1, 3).reshape(HEAD_DIM, width).astype(F32)
    output = jnp.dot(
        back.reshape(positions, inner), full_weight, preferred_element_type=F32
    ).astype(BF)
    return (output.reshape(upstream.shape), qkv_grad.reshape(qkv.shape), weight_grad)


def solution(mesh):
    in_specs = (
        P("dp", "seq", None, None),
        P("dp", None),
        P("dp", "seq", None, None),
        P("dp", None),
    )
    out_specs = (P("dp", "seq", None, None), P("dp", "seq", None, None), P("dp", None))
    return jax.shard_map(
        on_device, mesh=mesh, in_specs=in_specs, out_specs=out_specs, check_vma=False
    )
```

```python
import math

import jax
import jax.numpy as jnp
from jax import lax
from jax.experimental import pallas as pl
from jax.experimental.pallas import tpu as pltpu
from jax.sharding import PartitionSpec as P

HEAD_DIM = 72
HEADS = 8
NX, NY, NZ = 4, 8, 8
MESH = pl.DeviceIdType.MESH
BF, F32 = jnp.bfloat16, jnp.float32


def place():
    dp, seq = lax.axis_index("dp"), lax.axis_index("seq")
    zh, core = dp // 2, dp % 2
    zl, y, x = seq // 32, (seq // 4) % 8, seq % 4
    return zh, core, zl, y, x


def device(zh, core, zl, y, x):
    return (zh * 2 + core, zl * 32 + y * 4 + x)


def peers():
    zh, core, zl, y, x = place()

    def at_core():
        return device(zh, 1 - core, zl, y, x)

    def at_x(r):
        return device(zh, core, zl, y, (x + r) % NX)

    def at_y(r):
        return device(zh, core, zl, (y + r) % NY, x)

    def at_z(r):
        z = (zh * 2 + zl + r) % NZ
        return device(z // 2, core, z % 2, y, x)

    def at_plane(r):
        return device(zh, core, zl, (y + r // NX) % NY, (x + r % NX) % NX)

    def at_seq(k):
        i, c = k % 8, k // 8
        dy = 4 + (i // 2) * (1 - 2 * (i % 2)) - i % 2
        return device(zh, core, (zl + c // 4 + i) % 2, (y + dy) % NY, (x + c + i) % NX)

    return at_core, at_x, at_y, at_z, at_plane, at_seq


def exchange(src, dst, send_sem, recv_sem, keep_sem):
    _, _, _, _, _, at_seq = peers()
    me = lax.axis_index("seq")

    def start(r):
        to = at_seq(r)
        pltpu.make_async_remote_copy(
            src_ref=src.at[to[1]], dst_ref=dst.at[me], send_sem=send_sem, recv_sem=recv_sem,
            device_id=to, device_id_type=MESH,
        ).start()

    def keep():
        return pltpu.make_async_copy(src.at[me], dst.at[me], keep_sem)

    def finish():
        keep().wait()
        others = dst.at[pl.ds(0, NX * NY * 2 - 1)]
        pltpu.make_async_copy(others, others, recv_sem).wait()
        pltpu.make_async_copy(others, others, send_sem).wait()

    return start, keep, finish


def greet(barrier):
    at_core, _, _, at_z, _, at_seq = peers()
    pl.semaphore_signal(barrier, inc=1, device_id=at_core(), device_id_type=MESH)

    @pl.loop(1, NZ)
    def _(r):
        pl.semaphore_signal(barrier, inc=1, device_id=at_z(r), device_id_type=MESH)

    @pl.loop(48, 48 + 63)
    def _(k):
        pl.semaphore_signal(barrier, inc=1, device_id=at_seq(k % 64), device_id_type=MESH)


GREETED = 1 + (NZ - 1) + (NX * NY * 2 - 1)


def enter_kernel(
    qkv_in, up_in, w_ref, qkv_out, up_out, w_out,
    qkv_ref, up_ref, qs, qr, qk, us, ur, uk, wk, os, orr, zs, zr, xs, xr, cs, cr, ds, dr,
):
    zh, core, zl, y, x = place()
    dp = zh * 2 + core
    at_core = peers()[0]
    barrier = pltpu.get_barrier_semaphore()
    greet(barrier)
    q_start, q_keep, q_finish = exchange(qkv_ref, qkv_out, qs, qr, qk)
    u_start, u_keep, u_finish = exchange(up_ref, up_out, us, ur, uk)
    up_ref[...] = up_in[...].reshape(up_ref.shape)
    qkv_ref[...] = qkv_in[...].T.reshape(qkv_ref.shape)
    q_keep().start()
    u_keep().start()
    w_keep = pltpu.make_async_copy(w_ref, w_out.at[dp], wk)
    w_keep.start()
    pl.semaphore_wait(barrier, GREETED)

    def remote(src, dst, ss, rs, to):
        return pltpu.make_async_remote_copy(
            src_ref=src, dst_ref=dst, send_sem=ss, recv_sem=rs,
            device_id=to, device_id_type=MESH,
        )

    def over_z(r, part):
        to = device((zh + r) % 4, core, zl, y, x)
        return remote(w_ref.at[part], w_out.at[dp, part], zs.at[r - 1], zr.at[r - 1], to)

    def landed(r, part, sem):
        ref = w_out.at[((zh + 4 - r) % 4) * 2 + core, part]
        pltpu.make_async_copy(ref, ref, sem).wait()
        return ref

    def landed_core(r, part, sem):
        ref = w_out.at[((zh + 4 - r) % 4) * 2 + 1 - core, part]
        pltpu.make_async_copy(ref, ref, sem).wait()

    halves = (pl.ds(0, 5), pl.ds(5, 4))
    own_core = remote(w_ref, w_out.at[dp], os, orr, at_core())
    for half in (0, 1):
        @pl.when(x % 2 == half)
        def _(half=half):
            for r in (2, 1, 3):
                over_z(r, halves[half]).start()

    own_core.start()

    def send_in(low, high):
        @pl.loop(48 + low, 48 + high)
        def _(k):
            q_start(k % 64)
            u_start(k % 64)

    send_in(0, 63)
    across = device(zh, core, zl, y, x + 1 - 2 * (x % 2))
    for half in (0, 1):
        @pl.when(x % 2 == half)
        def _(half=half):
            mine, other = halves[half], halves[1 - half]
            for r in (1, 3, 2):
                ref = landed(r, mine, zr.at[r - 1])
                remote(ref, ref, xs.at[r - 1], xr.at[r - 1], across).start()
                remote(ref, ref, cs.at[r - 1], cr.at[r - 1], at_core()).start()

    for half in (0, 1):
        @pl.when(x % 2 == half)
        def _(half=half):
            mine, other = halves[half], halves[1 - half]
            for r in (1, 3, 2):
                ref = landed(r, other, xr.at[r - 1])
                remote(ref, ref, ds.at[r - 1], dr.at[r - 1], at_core()).start()
            for r in (1, 3, 2):
                over_z(r, mine).wait_send()
                landed(r, mine, xs.at[r - 1])
                landed(r, mine, cs.at[r - 1])
                landed(r, other, ds.at[r - 1])
                landed_core(r, mine, cr.at[r - 1])
                landed_core(r, other, dr.at[r - 1])

    own_core.wait()
    w_keep.wait()
    q_finish()
    u_finish()


def enter(qkv, up, weight, frames):
    dma = pltpu.SemaphoreType.DMA
    spec = pl.BlockSpec(memory_space=pltpu.VMEM)
    qkv_shape = (frames, qkv.shape[1] // frames, qkv.shape[0])
    up_shape = (frames, up.shape[0] // frames, up.shape[1])
    return pl.pallas_call(
        enter_kernel,
        out_shape=[
            jax.ShapeDtypeStruct(qkv_shape, BF),
            jax.ShapeDtypeStruct(up_shape, BF),
            jax.ShapeDtypeStruct((HEADS,) + weight.shape, BF),
        ],
        in_specs=[spec] * 3,
        out_specs=[spec] * 3,
        scratch_shapes=[pltpu.VMEM(qkv_shape, BF), pltpu.VMEM(up_shape, BF)]
        + [dma] * 9 + [dma((3,))] * 8,
        compiler_params=pltpu.CompilerParams(collective_id=0, has_side_effects=True),
        name="enter",
    )(qkv, up, weight)


def leave_kernel(
    grad_in, back_in, mixed_ref, up_ref, grad_out, back_out, out_ref,
    grad_ref, back_ref, gs, gr, gk, bs, br, bk,
    own0, rows0, cols0, snd1, rcv1, own1, snd2, rcv2, own2, snd3, rcv3, snd4, rcv4,
    s0, r0, t0, q0, s1, r1, s2, r2, s3, r3, s4, r4,
):
    zh, core, zl, y, x = place()
    at_core, at_x, at_y, at_z, at_plane, _ = peers()

    barrier = pltpu.get_barrier_semaphore()
    greet(barrier)
    g_start, g_keep, g_finish = exchange(grad_ref, grad_out, gs, gr, gk)
    b_start, b_keep, b_finish = exchange(back_ref, back_out, bs, br, bk)
    for p in range(grad_in.shape[0]):
        back_ref[:, p, :] = back_in[p]
        grad_ref[:, p, :] = grad_in[p]
    g_keep().start()
    b_keep().start()

    def add(rows, cols, first):
        for g in range(9):
            part = jnp.dot(
                rows[...], cols[:, g * 128:(g + 1) * 128], preferred_element_type=F32
            )
            for h in range(4):
                for rb in range(9):
                    u, at = rb * 9 + g, h * HEAD_DIM + rb * 8
                    spot = (u // 24, (u % 24) // 3, h, u % 3)
                    unit = part[at:at + 8]
                    own0[spot] = unit if first else own0[spot] + unit

    add(mixed_ref.at[core], up_ref, True)
    for h in range(4):
        for u in range(81, 96):
            own0[u // 24, (u % 24) // 3, h, u % 3] = jnp.zeros((8, 128), F32)
    pl.semaphore_wait(barrier, GREETED)

    def to_core(src, dst, ss, rs):
        return pltpu.make_async_remote_copy(
            src_ref=src, dst_ref=dst, send_sem=ss, recv_sem=rs,
            device_id=at_core(), device_id_type=MESH,
        )

    trade = (
        to_core(mixed_ref.at[1 - core], rows0, s0, r0),
        to_core(up_ref, cols0, t0, q0),
    )
    for copy in trade:
        copy.start()

    def send_back(low, high):
        @pl.loop(48 + low, 48 + high)
        def _(k):
            g_start(k % 64)
            b_start(k % 64)

    for copy in trade:
        copy.wait()
    add(rows0, cols0, False)

    def copy1(r):
        return pltpu.make_async_remote_copy(
            src_ref=snd1.at[r - 1], dst_ref=rcv1.at[r - 1],
            send_sem=s1.at[r - 1], recv_sem=r1.at[r - 1],
            device_id=at_x(r), device_id_type=MESH,
        )

    for r in (2, 1, 3):
        to = (x + r) % NX
        snd1[r - 1] = own0[to].astype(BF)
        copy1(r).start()
    send_back(0, 32)
    own1[...] = own0[x]
    for r in (1, 3, 2):
        copy1(r).wait()
    own1[...] = (own1[...] + rcv1[0].astype(F32)) + (rcv1[1].astype(F32) + rcv1[2].astype(F32))

    def copy2(r):
        return pltpu.make_async_remote_copy(
            src_ref=snd2.at[r - 1], dst_ref=rcv2.at[r - 1],
            send_sem=s2.at[r - 1], recv_sem=r2.at[r - 1],
            device_id=at_y(r), device_id_type=MESH,
        )

    for r in (4, 3, 5, 2, 6, 1, 7):
        snd2[r - 1] = own1[(y + r) % NY].astype(BF)
        copy2(r).start()
    send_back(32, 48)
    for r in (1, 7, 2, 6, 3, 5, 4):
        copy2(r).wait()
    total = own1[y]
    for r in range(NY - 1):
        total = total + rcv2[r].astype(F32)
    own2[...] = total

    def copy3(r):
        return pltpu.make_async_remote_copy(
            src_ref=snd3.at[r - 1], dst_ref=rcv3.at[r - 1],
            send_sem=s3.at[r - 1], recv_sem=r3.at[r - 1],
            device_id=at_z(r), device_id_type=MESH,
        )

    for r in (4, 3, 5, 2, 6, 1, 7):
        z = (zh * 2 + zl + r) % NZ
        snd3[r - 1] = own2[z // 2].astype(BF)
        copy3(r).start()
    send_back(48, 63)
    for r in (1, 7, 2, 6, 3, 5, 4):
        copy3(r).wait()
    total = own2[zh]
    for r in range(NZ - 1):
        total = total + rcv3[r].astype(F32)
    snd4[...] = (total * (1.0 / 256.0)).astype(BF)

    me = x * NY + y

    def copy4(r):
        return pltpu.make_async_remote_copy(
            src_ref=snd4, dst_ref=rcv4.at[me],
            send_sem=s4, recv_sem=r4,
            device_id=at_plane(r), device_id_type=MESH,
        )

    @pl.loop(1, NX * NY)
    def _(r):
        copy4(r).start()

    keep = pltpu.make_async_copy(snd4, rcv4.at[me], r4)
    keep.start()
    pltpu.make_async_copy(rcv4, rcv4, r4).wait()
    sent = rcv4.at[pl.ds(0, NX * NY - 1)]
    pltpu.make_async_copy(sent, sent, s4).wait()
    result = pltpu.make_async_copy(rcv4, out_ref, s4)
    result.start()
    result.wait()
    g_finish()
    b_finish()


def leave(grad, back, mixed_t, up):
    unit = (8, 128)
    grad_shape = (grad.shape[1], grad.shape[0], grad.shape[2])
    back_shape = (back.shape[1], back.shape[0], back.shape[2])
    vm = pltpu.VMEM
    dma = pltpu.SemaphoreType.DMA
    return pl.pallas_call(
        leave_kernel,
        out_shape=[
            jax.ShapeDtypeStruct(grad_shape, BF),
            jax.ShapeDtypeStruct(back_shape, BF),
            jax.ShapeDtypeStruct((32, 3, 8, 128), BF),
        ],
        in_specs=[pl.BlockSpec(memory_space=pltpu.VMEM)] * 4,
        out_specs=[pl.BlockSpec(memory_space=pltpu.VMEM)] * 3,
        scratch_shapes=[vm(grad_shape, BF), vm(back_shape, BF)] + [dma] * 6 + [
            vm((4, 8, 4, 3) + unit, F32),
            vm((4 * HEAD_DIM, up.shape[0]), BF),
            vm(up.shape, BF),
            vm((3, 8, 4, 3) + unit, BF),
            vm((3, 8, 4, 3) + unit, BF),
            vm((8, 4, 3) + unit, F32),
            vm((7, 4, 3) + unit, BF),
            vm((7, 4, 3) + unit, BF),
            vm((4, 3) + unit, F32),
            vm((7, 3) + unit, BF),
            vm((7, 3) + unit, BF),
            vm((3,) + unit, BF),
            vm((32, 3) + unit, BF),
            dma, dma, dma, dma,
            dma((3,)), dma((3,)),
            dma((7,)), dma((7,)),
            dma((7,)), dma((7,)),
            dma, dma,
        ],
        compiler_params=pltpu.CompilerParams(collective_id=1, has_side_effects=True),
        name="leave",
    )(grad, back, mixed_t, up)


def attend_all(stacked, grad_in, allowed, factor):
    frame_count, pos_here, _ = stacked.shape
    split = stacked.reshape(frame_count, pos_here, 3, HEADS, HEAD_DIM)
    queries, keys, values = split[:, :, 0], split[:, :, 1], split[:, :, 2]
    scores = jnp.einsum("fphd,gphd->phfg", queries, keys, preferred_element_type=F32) * factor
    scores = jnp.where(allowed, scores, F32(-1e30))
    exponent = jnp.exp(scores - jnp.max(scores, axis=-1, keepdims=True))
    attend = exponent / jnp.sum(exponent, axis=-1, keepdims=True)
    low = attend.astype(BF)
    mixed = jnp.einsum("phfg,gphd->fphd", low, values, preferred_element_type=F32).astype(BF)
    grad = grad_in.reshape(frame_count, pos_here, HEADS, HEAD_DIM)
    attend_grad = jnp.einsum("fphd,gphd->phfg", grad, values, preferred_element_type=F32)
    row_dot = jnp.sum(attend * attend_grad, axis=-1, keepdims=True)
    score_grad = (attend * (attend_grad - row_dot)).astype(BF)
    query_grad = (
        jnp.einsum("phfg,gphd->fphd", score_grad, keys, preferred_element_type=F32) * factor
    ).astype(BF)
    key_grad = (
        jnp.einsum("phfg,fphd->gphd", score_grad, queries, preferred_element_type=F32) * factor
    ).astype(BF)
    value_grad = jnp.einsum("phfg,fphd->gphd", low, grad, preferred_element_type=F32).astype(BF)
    packed = jnp.stack([query_grad, key_grad, value_grad], axis=2).transpose(1, 0, 2, 3, 4)
    return mixed, packed.reshape(pos_here, frame_count, 3 * HEADS * HEAD_DIM)


def on_device(qkv, segment_ids, upstream, out_weight):
    _, _, positions, packed = qkv.shape
    inner = HEADS * HEAD_DIM
    factor = 1.0 / math.sqrt(HEAD_DIM)
    width = out_weight.shape[1]
    frames = lax.axis_size("seq")
    pos_here = positions // frames
    stacked, up, full_weight = enter(
        qkv.reshape(positions, packed).T,
        upstream.reshape(positions, width),
        out_weight.reshape(HEAD_DIM // 8, 8, width),
        frames,
    )
    stacked, segment_ids = lax.optimization_barrier((stacked, segment_ids))
    allowed = (segment_ids[0, :, None] == segment_ids[0, None, :])[None, None]
    full_weight = full_weight.reshape(inner, width)
    up = up.reshape(frames * pos_here, width)

    grad_in = lax.dot_general(
        up, full_weight, (((1,), (1,)), ((), ())), preferred_element_type=F32
    ).astype(BF)
    mixed, packed_grad = attend_all(stacked, grad_in, allowed, factor)
    mixed_t = mixed.reshape(frames * pos_here, HEADS // 2, 2, HEAD_DIM)
    mixed_t = mixed_t.transpose(2, 1, 3, 0).reshape(2, inner // 2, frames * pos_here)
    back = mixed.transpose(1, 0, 2, 3).reshape(pos_here, frames, inner)
    qkv_grad, back, units = leave(packed_grad, back, mixed_t, up)
    units = units.reshape(96, 8, 128)[:81].reshape(9, 9, 8, 128)
    weight_grad = units.transpose(0, 2, 1, 3).reshape(HEAD_DIM, width).astype(F32)
    output = jnp.dot(
        back.reshape(positions, inner), full_weight, preferred_element_type=F32
    ).astype(BF)
    return (output.reshape(upstream.shape), qkv_grad.reshape(qkv.shape), weight_grad)


def solution(mesh):
    in_specs = (
        P("dp", "seq", None, None),
        P("dp", None),
        P("dp", "seq", None, None),
        P("dp", None),
    )
    out_specs = (P("dp", "seq", None, None), P("dp", "seq", None, None), P("dp", None))
    return jax.shard_map(
        on_device, mesh=mesh, in_specs=in_specs, out_specs=out_specs, check_vma=False
    )
```

```python
import math

import jax
import jax.numpy as jnp
from jax import lax
from jax.experimental import pallas as pl
from jax.experimental.pallas import tpu as pltpu
from jax.sharding import PartitionSpec as P

HEAD_DIM = 72
HEADS = 8
NX, NY, NZ = 4, 8, 8
MESH = pl.DeviceIdType.MESH
BF, F32 = jnp.bfloat16, jnp.float32


def place():
    dp, seq = lax.axis_index("dp"), lax.axis_index("seq")
    zh, core = dp // 2, dp % 2
    zl, y, x = seq // 32, (seq // 4) % 8, seq % 4
    return zh, core, zl, y, x


def device(zh, core, zl, y, x):
    return (zh * 2 + core, zl * 32 + y * 4 + x)


def peers():
    zh, core, zl, y, x = place()

    def at_core():
        return device(zh, 1 - core, zl, y, x)

    def at_x(r):
        return device(zh, core, zl, y, (x + r) % NX)

    def at_y(r):
        return device(zh, core, zl, (y + r) % NY, x)

    def at_z(r):
        z = (zh * 2 + zl + r) % NZ
        return device(z // 2, core, z % 2, y, x)

    def at_plane(r):
        return device(zh, core, zl, (y + r // NX) % NY, (x + r % NX) % NX)

    def at_seq(k):
        i, c = k % 8, k // 8
        dy = 4 + (i // 2) * (1 - 2 * (i % 2)) - i % 2
        return device(zh, core, (zl + c // 4 + i) % 2, (y + dy) % NY, (x + c + i) % NX)

    return at_core, at_x, at_y, at_z, at_plane, at_seq


def exchange(src, dst, send_sem, recv_sem, keep_sem):
    _, _, _, _, _, at_seq = peers()
    me = lax.axis_index("seq")

    def start(r):
        to = at_seq(r)
        pltpu.make_async_remote_copy(
            src_ref=src.at[to[1]], dst_ref=dst.at[me], send_sem=send_sem, recv_sem=recv_sem,
            device_id=to, device_id_type=MESH,
        ).start()

    def keep():
        return pltpu.make_async_copy(src.at[me], dst.at[me], keep_sem)

    def finish():
        keep().wait()
        others = dst.at[pl.ds(0, NX * NY * 2 - 1)]
        pltpu.make_async_copy(others, others, recv_sem).wait()
        pltpu.make_async_copy(others, others, send_sem).wait()

    return start, keep, finish


def greet(barrier):
    at_core, _, _, at_z, _, at_seq = peers()
    pl.semaphore_signal(barrier, inc=1, device_id=at_core(), device_id_type=MESH)

    @pl.loop(1, NZ)
    def _(r):
        pl.semaphore_signal(barrier, inc=1, device_id=at_z(r), device_id_type=MESH)

    @pl.loop(48, 48 + 63)
    def _(k):
        pl.semaphore_signal(barrier, inc=1, device_id=at_seq(k % 64), device_id_type=MESH)


GREETED = 1 + (NZ - 1) + (NX * NY * 2 - 1)


def enter_kernel(
    qkv_hbm, up_hbm, w_hbm, qkv_out, up_out, w_out,
    qkv_in, up_in, w_ref, load_sem, qkv_ref, up_ref, qs, qr, qk, us, ur, uk, wk, os, orr, zs, zr, xs, xr, cs, cr, ds, dr,
):
    zh, core, zl, y, x = place()
    dp = zh * 2 + core
    at_core = peers()[0]
    barrier = pltpu.get_barrier_semaphore()
    loads = [
        pltpu.make_async_copy(src, dst, load_sem.at[i])
        for i, (src, dst) in enumerate(
            ((up_hbm, up_in), (qkv_hbm, qkv_in), (w_hbm, w_ref))
        )
    ]
    for load in loads:
        load.start()
    greet(barrier)
    for load in loads:
        load.wait()
    q_start, q_keep, q_finish = exchange(qkv_ref, qkv_out, qs, qr, qk)
    u_start, u_keep, u_finish = exchange(up_ref, up_out, us, ur, uk)
    up_ref[...] = up_in[...].reshape(up_ref.shape)
    qkv_ref[...] = qkv_in[...].T.reshape(qkv_ref.shape)
    q_keep().start()
    u_keep().start()
    w_keep = pltpu.make_async_copy(w_ref, w_out.at[dp], wk)
    w_keep.start()
    pl.semaphore_wait(barrier, GREETED)

    def remote(src, dst, ss, rs, to):
        return pltpu.make_async_remote_copy(
            src_ref=src, dst_ref=dst, send_sem=ss, recv_sem=rs,
            device_id=to, device_id_type=MESH,
        )

    def over_z(r, part):
        to = device((zh + r) % 4, core, zl, y, x)
        return remote(w_ref.at[part], w_out.at[dp, part], zs.at[r - 1], zr.at[r - 1], to)

    def landed(r, part, sem):
        ref = w_out.at[((zh + 4 - r) % 4) * 2 + core, part]
        pltpu.make_async_copy(ref, ref, sem).wait()
        return ref

    def landed_core(r, part, sem):
        ref = w_out.at[((zh + 4 - r) % 4) * 2 + 1 - core, part]
        pltpu.make_async_copy(ref, ref, sem).wait()

    halves = (pl.ds(0, 5), pl.ds(5, 4))
    own_core = remote(w_ref, w_out.at[dp], os, orr, at_core())
    for half in (0, 1):
        @pl.when(x % 2 == half)
        def _(half=half):
            for r in (2, 1, 3):
                over_z(r, halves[half]).start()

    own_core.start()

    def send_in(low, high):
        @pl.loop(48 + low, 48 + high)
        def _(k):
            q_start(k % 64)
            u_start(k % 64)

    send_in(0, 63)
    across = device(zh, core, zl, y, x + 1 - 2 * (x % 2))
    for half in (0, 1):
        @pl.when(x % 2 == half)
        def _(half=half):
            mine, other = halves[half], halves[1 - half]
            for r in (1, 3, 2):
                ref = landed(r, mine, zr.at[r - 1])
                remote(ref, ref, xs.at[r - 1], xr.at[r - 1], across).start()
                remote(ref, ref, cs.at[r - 1], cr.at[r - 1], at_core()).start()

    for half in (0, 1):
        @pl.when(x % 2 == half)
        def _(half=half):
            mine, other = halves[half], halves[1 - half]
            for r in (1, 3, 2):
                ref = landed(r, other, xr.at[r - 1])
                remote(ref, ref, ds.at[r - 1], dr.at[r - 1], at_core()).start()
            for r in (1, 3, 2):
                over_z(r, mine).wait_send()
                landed(r, mine, xs.at[r - 1])
                landed(r, mine, cs.at[r - 1])
                landed(r, other, ds.at[r - 1])
                landed_core(r, mine, cr.at[r - 1])
                landed_core(r, other, dr.at[r - 1])

    own_core.wait()
    w_keep.wait()
    q_finish()
    u_finish()


def enter(qkv, up, weight, frames):
    dma = pltpu.SemaphoreType.DMA
    spec = pl.BlockSpec(memory_space=pltpu.VMEM)
    qkv_shape = (frames, qkv.shape[1] // frames, qkv.shape[0])
    up_shape = (frames, up.shape[0] // frames, up.shape[1])
    return pl.pallas_call(
        enter_kernel,
        out_shape=[
            jax.ShapeDtypeStruct(qkv_shape, BF),
            jax.ShapeDtypeStruct(up_shape, BF),
            jax.ShapeDtypeStruct((HEADS,) + weight.shape, BF),
        ],
        in_specs=[pl.BlockSpec(memory_space=pltpu.HBM)] * 3,
        out_specs=[spec] * 3,
        scratch_shapes=[
            pltpu.VMEM(qkv.shape, BF), pltpu.VMEM(up.shape, BF), pltpu.VMEM(weight.shape, BF),
            dma((3,)),
        ] + [pltpu.VMEM(qkv_shape, BF), pltpu.VMEM(up_shape, BF)]
        + [dma] * 9 + [dma((3,))] * 8,
        compiler_params=pltpu.CompilerParams(collective_id=0, has_side_effects=True),
        name="enter",
    )(qkv, up, weight)


def leave_kernel(
    grad_in, back_in, mixed_ref, up_ref, w_ref, grad_res, res_ref, out_ref,
    grad_ref, back_ref, grad_out, back_out, gs, gr, gk, bs, br, bk,
    own0, rows0, cols0, snd1, rcv1, own1, snd2, rcv2, own2, snd3, rcv3, snd4, rcv4,
    s0, r0, t0, q0, s1, r1, s2, r2, s3, r3, s4, r4,
):
    zh, core, zl, y, x = place()
    at_core, at_x, at_y, at_z, at_plane, _ = peers()

    barrier = pltpu.get_barrier_semaphore()
    greet(barrier)
    g_start, g_keep, g_finish = exchange(grad_ref, grad_out, gs, gr, gk)
    b_start, b_keep, b_finish = exchange(back_ref, back_out, bs, br, bk)
    for p in range(grad_in.shape[0]):
        back_ref[:, p, :] = back_in[p]
        grad_ref[:, p, :] = grad_in[p]
    g_keep().start()
    b_keep().start()

    def add(rows, cols, first):
        for g in range(9):
            part = jnp.dot(
                rows[...], cols[:, g * 128:(g + 1) * 128], preferred_element_type=F32
            )
            for h in range(4):
                for rb in range(9):
                    u, at = rb * 9 + g, h * HEAD_DIM + rb * 8
                    spot = (u // 24, (u % 24) // 3, h, u % 3)
                    unit = part[at:at + 8]
                    own0[spot] = unit if first else own0[spot] + unit

    add(mixed_ref.at[core], up_ref, True)
    for h in range(4):
        for u in range(81, 96):
            own0[u // 24, (u % 24) // 3, h, u % 3] = jnp.zeros((8, 128), F32)
    pl.semaphore_wait(barrier, GREETED)

    def to_core(src, dst, ss, rs):
        return pltpu.make_async_remote_copy(
            src_ref=src, dst_ref=dst, send_sem=ss, recv_sem=rs,
            device_id=at_core(), device_id_type=MESH,
        )

    trade = (
        to_core(mixed_ref.at[1 - core], rows0, s0, r0),
        to_core(up_ref, cols0, t0, q0),
    )
    for copy in trade:
        copy.start()

    def send_back(low, high):
        @pl.loop(48 + low, 48 + high)
        def _(k):
            g_start(k % 64)
            b_start(k % 64)

    for copy in trade:
        copy.wait()
    add(rows0, cols0, False)

    def copy1(r):
        return pltpu.make_async_remote_copy(
            src_ref=snd1.at[r - 1], dst_ref=rcv1.at[r - 1],
            send_sem=s1.at[r - 1], recv_sem=r1.at[r - 1],
            device_id=at_x(r), device_id_type=MESH,
        )

    for r in (2, 1, 3):
        to = (x + r) % NX
        snd1[r - 1] = own0[to].astype(BF)
        copy1(r).start()
    send_back(0, 32)
    own1[...] = own0[x]
    for r in (1, 3, 2):
        copy1(r).wait()
    own1[...] = (own1[...] + rcv1[0].astype(F32)) + (rcv1[1].astype(F32) + rcv1[2].astype(F32))

    def copy2(r):
        return pltpu.make_async_remote_copy(
            src_ref=snd2.at[r - 1], dst_ref=rcv2.at[r - 1],
            send_sem=s2.at[r - 1], recv_sem=r2.at[r - 1],
            device_id=at_y(r), device_id_type=MESH,
        )

    for r in (4, 3, 5, 2, 6, 1, 7):
        snd2[r - 1] = own1[(y + r) % NY].astype(BF)
        copy2(r).start()
    send_back(32, 48)
    for r in (1, 7, 2, 6, 3, 5, 4):
        copy2(r).wait()
    total = own1[y]
    for r in range(NY - 1):
        total = total + rcv2[r].astype(F32)
    own2[...] = total

    def copy3(r):
        return pltpu.make_async_remote_copy(
            src_ref=snd3.at[r - 1], dst_ref=rcv3.at[r - 1],
            send_sem=s3.at[r - 1], recv_sem=r3.at[r - 1],
            device_id=at_z(r), device_id_type=MESH,
        )

    for r in (4, 3, 5, 2, 6, 1, 7):
        z = (zh * 2 + zl + r) % NZ
        snd3[r - 1] = own2[z // 2].astype(BF)
        copy3(r).start()
    send_back(48, 63)
    for r in (1, 7, 2, 6, 3, 5, 4):
        copy3(r).wait()
    total = own2[zh]
    for r in range(NZ - 1):
        total = total + rcv3[r].astype(F32)
    snd4[...] = (total * (1.0 / 256.0)).astype(BF)

    me = x * NY + y

    def copy4(r):
        return pltpu.make_async_remote_copy(
            src_ref=snd4, dst_ref=rcv4.at[me],
            send_sem=s4, recv_sem=r4,
            device_id=at_plane(r), device_id_type=MESH,
        )

    @pl.loop(1, NX * NY)
    def _(r):
        copy4(r).start()

    keep = pltpu.make_async_copy(snd4, rcv4.at[me], r4)
    keep.start()
    b_finish()
    flat = back_out[...].reshape(res_ref.shape[0], w_ref.shape[0])
    for g in range(0, 1152, 384):
        res_ref[:, g:g + 384] = jnp.dot(
            flat, w_ref[:, g:g + 384], preferred_element_type=F32
        ).astype(BF)
    g_finish()
    grad_res[...] = grad_out[...].reshape(grad_res.shape[1], grad_res.shape[0]).T
    pltpu.make_async_copy(rcv4, rcv4, r4).wait()
    sent = rcv4.at[pl.ds(0, NX * NY - 1)]
    pltpu.make_async_copy(sent, sent, s4).wait()
    result = pltpu.make_async_copy(rcv4, out_ref, s4)
    result.start()
    result.wait()


def leave(grad, back, mixed_t, up, weight):
    unit = (8, 128)
    grad_shape = (grad.shape[1], grad.shape[0], grad.shape[2])
    back_shape = (back.shape[1], back.shape[0], back.shape[2])
    vm = pltpu.VMEM
    dma = pltpu.SemaphoreType.DMA
    return pl.pallas_call(
        leave_kernel,
        out_shape=[
            jax.ShapeDtypeStruct((grad.shape[2], up.shape[0]), BF),
            jax.ShapeDtypeStruct(up.shape, BF),
            jax.ShapeDtypeStruct((32, 3, 8, 128), BF),
        ],
        in_specs=[pl.BlockSpec(memory_space=pltpu.VMEM)] * 5,
        out_specs=[pl.BlockSpec(memory_space=pltpu.VMEM)] * 3,
        scratch_shapes=[vm(grad_shape, BF), vm(back_shape, BF)] * 2 + [dma] * 6 + [
            vm((4, 8, 4, 3) + unit, F32),
            vm((4 * HEAD_DIM, up.shape[0]), BF),
            vm(up.shape, BF),
            vm((3, 8, 4, 3) + unit, BF),
            vm((3, 8, 4, 3) + unit, BF),
            vm((8, 4, 3) + unit, F32),
            vm((7, 4, 3) + unit, BF),
            vm((7, 4, 3) + unit, BF),
            vm((4, 3) + unit, F32),
            vm((7, 3) + unit, BF),
            vm((7, 3) + unit, BF),
            vm((3,) + unit, BF),
            vm((32, 3) + unit, BF),
            dma, dma, dma, dma,
            dma((3,)), dma((3,)),
            dma((7,)), dma((7,)),
            dma((7,)), dma((7,)),
            dma, dma,
        ],
        compiler_params=pltpu.CompilerParams(collective_id=1, has_side_effects=True, vmem_limit_bytes=16 * 2**20),
        name="leave",
    )(grad, back, mixed_t, up, weight)


def attend_all(stacked, grad_in, allowed, factor):
    frame_count, pos_here, _ = stacked.shape
    split = stacked.reshape(frame_count, pos_here, 3, HEADS, HEAD_DIM)
    queries, keys, values = split[:, :, 0], split[:, :, 1], split[:, :, 2]
    scores = jnp.einsum("fphd,gphd->phfg", queries, keys, preferred_element_type=F32) * factor
    scores = jnp.where(allowed, scores, F32(-1e30))
    exponent = jnp.exp(scores - jnp.max(scores, axis=-1, keepdims=True))
    attend = exponent / jnp.sum(exponent, axis=-1, keepdims=True)
    low = attend.astype(BF)
    mixed = jnp.einsum("phfg,gphd->fphd", low, values, preferred_element_type=F32).astype(BF)
    grad = grad_in.reshape(frame_count, pos_here, HEADS, HEAD_DIM)
    attend_grad = jnp.einsum("fphd,gphd->phfg", grad, values, preferred_element_type=F32)
    row_dot = jnp.sum(attend * attend_grad, axis=-1, keepdims=True)
    score_grad = (attend * (attend_grad - row_dot)).astype(BF)
    query_grad = (
        jnp.einsum("phfg,gphd->fphd", score_grad, keys, preferred_element_type=F32) * factor
    ).astype(BF)
    key_grad = (
        jnp.einsum("phfg,fphd->gphd", score_grad, queries, preferred_element_type=F32) * factor
    ).astype(BF)
    value_grad = jnp.einsum("phfg,fphd->gphd", low, grad, preferred_element_type=F32).astype(BF)
    packed = jnp.stack([query_grad, key_grad, value_grad], axis=2).transpose(1, 0, 2, 3, 4)
    return mixed, packed.reshape(pos_here, frame_count, 3 * HEADS * HEAD_DIM)


def on_device(qkv, segment_ids, upstream, out_weight):
    _, _, positions, packed = qkv.shape
    inner = HEADS * HEAD_DIM
    factor = 1.0 / math.sqrt(HEAD_DIM)
    width = out_weight.shape[1]
    frames = lax.axis_size("seq")
    pos_here = positions // frames
    stacked, up, full_weight = enter(
        qkv.reshape(positions, packed).T,
        upstream.reshape(positions, width),
        out_weight.reshape(HEAD_DIM // 8, 8, width),
        frames,
    )
    stacked, segment_ids = lax.optimization_barrier((stacked, segment_ids))
    allowed = (segment_ids[0, :, None] == segment_ids[0, None, :])[None, None]
    full_weight = full_weight.reshape(inner, width)
    up = up.reshape(frames * pos_here, width)

    grad_in = lax.dot_general(
        up, full_weight, (((1,), (1,)), ((), ())), preferred_element_type=F32
    ).astype(BF)
    mixed, packed_grad = attend_all(stacked, grad_in, allowed, factor)
    mixed_t = mixed.reshape(frames * pos_here, HEADS // 2, 2, HEAD_DIM)
    mixed_t = mixed_t.transpose(2, 1, 3, 0).reshape(2, inner // 2, frames * pos_here)
    back = mixed.transpose(1, 0, 2, 3).reshape(pos_here, frames, inner)
    qkv_grad, output, units = leave(packed_grad, back, mixed_t, up, full_weight)
    units = units.reshape(96, 8, 128)[:81].reshape(9, 9, 8, 128)
    weight_grad = units.transpose(0, 2, 1, 3).reshape(HEAD_DIM, width).astype(F32)
    return (output.reshape(upstream.shape), qkv_grad.T.reshape(qkv.shape), weight_grad)


def solution(mesh):
    in_specs = (
        P("dp", "seq", None, None),
        P("dp", None),
        P("dp", "seq", None, None),
        P("dp", None),
    )
    out_specs = (P("dp", "seq", None, None), P("dp", "seq", None, None), P("dp", None))
    return jax.shard_map(
        on_device, mesh=mesh, in_specs=in_specs, out_specs=out_specs, check_vma=False
    )
```
